32 devices in a mesh: row: 4 (over y, core), col: 8 (over z, x).
Axes of the slice: x: 2, y: 2, z: 4, core: 2. Of those that a mesh axis runs over, the one named last changes fastest.
Arguments:
- positions: float32 [512, 147], P(('row', 'col')), may hold values from -0.55 to 9.45, as said below
- coefficients: float32 [512, 147], P(('row', 'col')), may hold values from -6 to 6
- atom_pairs: int32 [2, 1176], replicated, may hold values from 0 to 48, as said below
- pair_scale: float32 [1176], replicated, may hold values from 0.5 to 2
Outputs:
- applied: float32 [512, 147], P(('row', 'col'))
The draws below stay inside these ranges and needn't reach their ends.
Inputs may be any that keep to these rules, and one draw needn't show every extreme that they name: `atom_pairs`: every unordered pair of two different atoms stands in exactly one column, the smaller atom in row 0. `positions`: every two atoms of a geometry lie 0.6 or more apart; all geometries are displacements of one molecule.
All inputs are finite; a program needn't handle non-finite values.
Results may differ from the reference program's by a relative error of at most 0.0003.
Values sent between devices are 32-bit elements; how exact they have to be, the bound alone decides.
A program may use at most 64 MiB of HBM per device.

```python
import math
import jax
import jax.numpy as jnp
import numpy as np
from jax import lax

ATOMS = 49
FEATURES = 1176
GEOMS = 512


def draw_positions(key, part):
    base_key = jax.random.fold_in(key, 11)
    move_key = jax.random.fold_in(key, 12)
    lift_key = jax.random.fold_in(key, 13)
    atom_ids = jnp.arange(ATOMS, dtype=jnp.int32)
    grid = jnp.stack([(atom_ids % 7).astype(jnp.float32) * 1.5, (atom_ids // 7).astype(jnp.float32) * 1.5, jnp.zeros((ATOMS,), jnp.float32)], 0)
    jitter = jax.random.uniform(base_key, (3, ATOMS), jnp.float32, -1.0, 1.0) * jnp.array([0.2, 0.2, 0.3], jnp.float32)[:, None]
    planar = jax.random.uniform(move_key, (GEOMS, 2, ATOMS), jnp.float32, -0.25, 0.25)
    lifted = jax.random.uniform(lift_key, (GEOMS, 1, ATOMS), jnp.float32, -0.25, 3.0)
    moves = jnp.concatenate([planar, lifted], axis=1)
    return ((grid + jitter)[None] + moves).reshape(GEOMS, 3 * ATOMS)


def draw_atom_pairs(key, part):
    first, second = np.triu_indices(ATOMS, 1)
    table = jnp.asarray(np.stack([first, second]).astype(np.int32))
    order = jax.random.permutation(jax.random.fold_in(key, 21), FEATURES)
    return table[:, order]


def level_of(key, extent, cuts, smallest, largest):
    def one(dim, shards_of):
        heights = jax.random.uniform(jax.random.fold_in(jax.random.fold_in(key, 6), dim), (shards_of,), jnp.float32, smallest / len(cuts), largest / len(cuts))
        return jnp.repeat(jnp.exp(heights), extent[dim] // shards_of).reshape((-1,) + (1,) * (len(extent) - dim - 1))

    factor_of = one(*cuts[0])
    for cut in cuts[1:]:
        factor_of = factor_of * one(*cut)
    return factor_of


def gaussian(key, shape, deviation, bound, cuts=(), kind=jnp.bfloat16):
    factor_of = level_of(key, shape, cuts, -0.22, 0.18) if cuts else 1.0
    values = jax.random.normal(key, shape, jnp.float32) * deviation * factor_of
    return jnp.minimum(jnp.maximum(values, -bound), bound).astype(kind)


def setup_inputs(seed: int = 0) -> dict:
    arg_keys = jax.random.split(jax.random.key(seed), 5)
    return {
        "positions": draw_positions(jax.random.fold_in(arg_keys[4], 71), 0),
        "coefficients": gaussian(arg_keys[1], (GEOMS, 3 * ATOMS), 1.0, 6.0, ((0, 32),), jnp.float32),
        "atom_pairs": draw_atom_pairs(jax.random.fold_in(arg_keys[4], 71), 0),
        "pair_scale": jnp.clip(jnp.exp(jax.random.uniform(arg_keys[3], (FEATURES,), jnp.float32, math.log(0.5), math.log(2.0))), 0.5, 2.0),
    }


highest = lax.Precision.HIGHEST
length_scale = 2.0
decay_rate = math.sqrt(5.0) / length_scale
outer_factor = decay_rate * decay_rate / 3.0
radial_factor = decay_rate * decay_rate

def pair_table(atom_pairs, atoms):
    atom_ids = jnp.arange(atoms, dtype=jnp.int32)[:, None]
    first = (atom_ids == atom_pairs[0][None, :]).astype(jnp.float32)
    second = (atom_ids == atom_pairs[1][None, :]).astype(jnp.float32)
    return first - second

def geometry_terms(positions, coefficients, onehot, pair_scale):
    count = positions.shape[0]
    atoms = onehot.shape[0]
    spans = jnp.dot(positions.reshape(count * 3, atoms), onehot, precision=highest).reshape(count, 3, -1)
    moves = jnp.dot(coefficients.reshape(count * 3, atoms), onehot, precision=highest).reshape(count, 3, -1)
    inverse = 1.0 / jnp.sqrt(lax.optimization_barrier(jnp.sum(spans * spans, axis=1)))
    features = pair_scale[None, :] * inverse
    weights = features * inverse * inverse
    tangents = -weights * lax.optimization_barrier(jnp.sum(spans * moves, axis=1))
    return (features, tangents, spans, weights)

def pull_back(grads, spans, weights, onehot):
    count = grads.shape[0]
    terms = -(weights * grads)[:, None, :] * spans
    return jnp.dot(terms.reshape(count * 3, -1), onehot.T, precision=highest).reshape(count, -1)

def kernel_terms(rows_x, cols_x):
    gram = jnp.dot(rows_x, cols_x.T, precision=highest)
    sq_dist = lax.optimization_barrier(jnp.sum(rows_x * rows_x, axis=1))[:, None] + lax.optimization_barrier(jnp.sum(cols_x * cols_x, axis=1))[None, :] - 2.0 * gram
    radius = jnp.sqrt(jnp.maximum(sq_dist, 0.0))
    envelope = outer_factor * jnp.exp(-decay_rate * radius)
    return (envelope, envelope * (1.0 + decay_rate * radius))

def row_apply(rows_x, rows_u, cols_x, cols_u):
    envelope, direct = kernel_terms(rows_x, cols_x)
    cross = jnp.dot(rows_x, cols_u.T, precision=highest) - lax.optimization_barrier(jnp.sum(cols_x * cols_u, axis=1))[None, :]
    bent = envelope * cross
    return jnp.dot(direct, cols_u, precision=highest) - radial_factor * (lax.optimization_barrier(jnp.sum(bent, axis=1))[:, None] * rows_x - jnp.dot(bent, cols_x, precision=highest))

def reference(positions, coefficients, atom_pairs, pair_scale):
    total = positions.shape[0]
    atoms = positions.shape[1] // 3
    onehot = pair_table(atom_pairs, atoms)
    features, tangents, spans, weights = geometry_terms(positions, coefficients, onehot, pair_scale)
    block = math.gcd(total, 512)
    width = features.shape[1]

    def one_block(pieces):
        return row_apply(pieces[0], pieces[1], features, tangents)
    grads = lax.map(one_block, (features.reshape(total // block, block, width), tangents.reshape(total // block, block, width)))
    return pull_back(grads.reshape(total, width), spans, weights, onehot)
```

```python
import functools
import math

import jax
import jax.numpy as jnp
from jax import lax
from jax.experimental import pallas as pl
from jax.experimental.pallas import tpu as pltpu
from jax.sharding import PartitionSpec as P

length_scale = 2.0
decay_rate = math.sqrt(5.0) / length_scale
outer_factor = decay_rate * decay_rate / 3.0
radial_factor = decay_rate * decay_rate

LANES = 128
HALF = 64
TILE = 256
f32, bf16 = jnp.float32, jnp.bfloat16


def dot(a, b):
    return jnp.dot(a, b, preferred_element_type=f32)


def rounded(v):
    return v.astype(bf16).astype(f32)


def two_parts(v):
    hi = v.astype(bf16)
    return hi, (v - hi.astype(f32)).astype(bf16)


def operands(packed):
    hi = rounded(packed)
    rest = packed - hi
    mid = rounded(rest)
    low = pltpu.roll(rest - mid, HALF, 1)
    first = lax.broadcasted_iota(jnp.int32, packed.shape, 1) < HALF
    hi = hi.astype(bf16)
    for_spans = jnp.concatenate([hi, jnp.where(first, mid, low).astype(bf16)], axis=1)
    for_moves = jnp.concatenate([hi, jnp.where(first, low, mid).astype(bf16)], axis=1)
    return for_spans, for_moves


def kernel(
    row_count, col_count, per, atoms, width,
    pos_ref, coef_ref, pairs_ref, scale_ref, out_ref,
    gathered, pairs, scale, table_s, table_m, own_s, own_x, own_w, own_t, hold_x, hold_u, acc, bent_sum,
    send_col, recv_col, send_row, recv_row,
):
    row = lax.axis_index("row")
    col = lax.axis_index("col")
    padded = table_s.shape[1]
    block = 3 * per
    count = col_count * per
    halves = row_count // 2 if row_count % 2 == 0 else row_count
    cores = row_count // halves

    def row_peer(k, sign):
        ky, kc = k // cores, k % cores
        y, c = row // cores, row % cores
        if sign > 0:
            return lax.rem(y + ky, halves) * cores + lax.rem(c + kc, cores)
        return lax.rem(y + halves - ky, halves) * cores + lax.rem(c + cores - kc, cores)

    barrier = pltpu.get_barrier_semaphore()
    for s in range(1, col_count):
        pl.semaphore_signal(
            barrier, inc=1, device_id=(row, lax.rem(col + s, col_count)), device_id_type=pl.DeviceIdType.MESH
        )
    for k in range(1, row_count):
        pl.semaphore_signal(
            barrier, inc=1, device_id=(row_peer(k, 1), col), device_id_type=pl.DeviceIdType.MESH
        )

    position, coefficient = pos_ref[...], coef_ref[...]
    gap = jnp.zeros((per, HALF - atoms), f32)
    for k in range(3):
        cut = slice(k * atoms, (k + 1) * atoms)
        gathered[0, k * per : (k + 1) * per, :] = jnp.concatenate(
            [position[:, cut], gap, coefficient[:, cut], gap], axis=1
        )
    pl.semaphore_wait(barrier, col_count - 1 + row_count - 1)

    spread = []
    for s in range(1, col_count):
        spread.append(
            pltpu.make_async_remote_copy(
                src_ref=gathered.at[0, pl.ds(0, block)],
                dst_ref=gathered.at[0, pl.ds(s * block, block)],
                send_sem=send_col.at[s],
                recv_sem=recv_col.at[s],
                device_id=(row, lax.rem(col + col_count - s, col_count)),
                device_id_type=pl.DeviceIdType.MESH,
            )
        )
    for copy in spread:
        copy.start()

    pairs[...] = jnp.full(pairs.shape, -1, jnp.int32)
    pairs[0:2, 0:width] = pairs_ref[...]
    scale[...] = jnp.zeros(scale.shape, f32)
    scale[0:1, 0:width] = scale_ref[...]
    ids = lax.broadcasted_iota(jnp.int32, (HALF, padded), 0)
    signs = (jnp.where(ids == pairs[0:1, :], 1.0, 0.0) - jnp.where(ids == pairs[1:2, :], 1.0, 0.0)).astype(bf16)
    blank = jnp.zeros((HALF, padded), bf16)
    for q in range(4):
        table_s[q * HALF : (q + 1) * HALF, :] = blank if q == 1 else signs
        table_m[q * HALF : (q + 1) * HALF, :] = blank if q == 0 else signs

    def terms(for_spans, for_moves, geoms, t):
        cut = slice(t * TILE, (t + 1) * TILE)
        spans = dot(for_spans, table_s[:, cut]).reshape(geoms, 3, per, TILE)
        moves = dot(for_moves, table_m[:, cut]).reshape(geoms, 3, per, TILE)
        square = spans[:, 0] * spans[:, 0] + spans[:, 1] * spans[:, 1] + spans[:, 2] * spans[:, 2]
        inner = spans[:, 0] * moves[:, 0] + spans[:, 1] * moves[:, 1] + spans[:, 2] * moves[:, 2]
        square = square.reshape(geoms * per, TILE)
        inner = inner.reshape(geoms * per, TILE)
        if (t + 1) * TILE > width:
            lane = lax.broadcasted_iota(jnp.int32, square.shape, 1)
            square = jnp.where(lane < width - t * TILE, square, 1.0)
        inverse = lax.rsqrt(square)
        features = scale[0:1, cut] * inverse
        weights = features * inverse * inverse
        return spans, features, weights, -weights * inner

    for_spans, for_moves = operands(gathered[0, 0:block, :])
    own_square = jnp.zeros((per, 1), f32)
    for t in range(padded // TILE):
        cut = slice(t * TILE, (t + 1) * TILE)
        spans, features, weights, _ = terms(for_spans, for_moves, 1, t)
        own_s[:, cut] = spans.reshape(block, TILE)
        own_x[:, cut] = features
        own_w[:, cut] = weights
        own_square += jnp.sum(features * features, axis=1, keepdims=True)
        hi = rounded(features)
        stacked = jnp.concatenate([hi, features - hi, jnp.zeros((LANES - 2 * per, TILE), f32)], axis=0)
        own_t[cut, :] = stacked.T.astype(bf16)
    acc[...] = jnp.zeros(acc.shape, f32)
    bent_sum[...] = jnp.zeros(bent_sum.shape, f32)

    for copy in spread:
        copy.wait_recv()
    pushed = []
    for k in range(1, row_count):
        pushed.append(
            pltpu.make_async_remote_copy(
                src_ref=gathered.at[0],
                dst_ref=gathered.at[k],
                send_sem=send_row.at[k],
                recv_sem=recv_row.at[k],
                device_id=(row_peer(k, -1), col),
                device_id_type=pl.DeviceIdType.MESH,
            )
        )
    for copy in pushed:
        copy.start()

    def one_chunk(k, carry):
        @pl.when(k > 0)
        def _():
            pltpu.make_async_remote_copy(
                src_ref=gathered.at[0],
                dst_ref=gathered.at[k],
                send_sem=send_row.at[k],
                recv_sem=recv_row.at[k],
                device_id=(row, col),
                device_id_type=pl.DeviceIdType.MESH,
            ).wait_recv()

        for_spans, for_moves = operands(gathered[k])
        square = jnp.zeros((count, LANES), f32)
        mixed = jnp.zeros((count, LANES), f32)
        for t in range(padded // TILE):
            cut = slice(t * TILE, (t + 1) * TILE)
            _, features, _, tangents = terms(for_spans, for_moves, col_count, t)
            for part in range(TILE // LANES):
                x = features[:, part * LANES : (part + 1) * LANES]
                u = tangents[:, part * LANES : (part + 1) * LANES]
                square += x * x
                mixed += x * u
            hi, low = two_parts(features)
            hold_x[0:count, cut] = hi
            hold_x[count : 2 * count, cut] = low
            hi, low = two_parts(tangents)
            hold_u[0:count, cut] = hi
            hold_u[count : 2 * count, cut] = low
        turned = own_t[...]
        gram = dot(hold_x[...], turned)
        gram = (gram[0:count] + gram[count : 2 * count]).T
        gram = gram[0:per] + gram[per : 2 * per]
        cross = dot(hold_u[...], turned)
        cross = (cross[0:count] + cross[count : 2 * count]).T
        cross = cross[0:per] + cross[per : 2 * per]
        square = jnp.sum(square.T, axis=0, keepdims=True)
        mixed = jnp.sum(mixed.T, axis=0, keepdims=True)
        radius = jnp.sqrt(jnp.maximum(own_square + square - 2.0 * gram, 0.0))
        envelope = outer_factor * jnp.exp(-decay_rate * radius)
        direct = envelope * (1.0 + decay_rate * radius)
        bent = radial_factor * (envelope * (cross - mixed))
        bent_sum[...] += jnp.broadcast_to(jnp.sum(bent, axis=1, keepdims=True), bent_sum.shape)

        def doubled(v):
            hi = rounded(v)
            both = jnp.concatenate([hi, v - hi], axis=0).astype(bf16)
            return jnp.concatenate([both, both], axis=1)

        acc[...] += dot(doubled(direct), hold_u[...]) + dot(doubled(bent), hold_x[...])
        return carry

    lax.fori_loop(0, row_count, one_chunk, 0)

    grads = acc[0:per, :] + acc[per : 2 * per, :] - bent_sum[:, 0:1] * own_x[...]
    pulled = -(own_w[...] * grads)
    pieces = []
    for k in range(3):
        pieces.append(pulled * own_s[k * per : (k + 1) * per, :])
    whole = jnp.concatenate(pieces, axis=0)
    hi = rounded(whole)
    mid = rounded(whole - hi)
    stacked = jnp.concatenate([hi, mid, whole - hi - mid], axis=0).astype(bf16)
    result = lax.dot_general(
        stacked, table_s[0:LANES, :], (((1,), (1,)), ((), ())), preferred_element_type=f32
    )
    result = result[0:block] + result[block : 2 * block] + result[2 * block : 3 * block]
    out_ref[...] = jnp.concatenate([result[k * per : (k + 1) * per, 0:atoms] for k in range(3)], axis=1)
    for copy in spread + pushed:
        copy.wait_send()


def on_device(positions, coefficients, atom_pairs, pair_scale):
    row_count = lax.axis_size("row")
    col_count = lax.axis_size("col")
    per = positions.shape[0]
    atoms = positions.shape[1] // 3
    width = atom_pairs.shape[1]
    padded = -(-width // TILE) * TILE
    count = col_count * per
    vmem = pl.BlockSpec(memory_space=pltpu.VMEM)
    return pl.pallas_call(
        functools.partial(kernel, row_count, col_count, per, atoms, width),
        out_shape=jax.ShapeDtypeStruct(positions.shape, f32),
        in_specs=[vmem] * 4,
        out_specs=vmem,
        scratch_shapes=[
            pltpu.VMEM((row_count, col_count * 3 * per, LANES), f32),
            pltpu.VMEM((8, padded), jnp.int32),
            pltpu.VMEM((8, padded), f32),
            pltpu.VMEM((TILE, padded), bf16),
            pltpu.VMEM((TILE, padded), bf16),
            pltpu.VMEM((3 * per, padded), f32),
            pltpu.VMEM((per, padded), f32),
            pltpu.VMEM((per, padded), f32),
            pltpu.VMEM((padded, LANES), bf16),
            pltpu.VMEM((2 * count, padded), bf16),
            pltpu.VMEM((2 * count, padded), bf16),
            pltpu.VMEM((2 * per, padded), f32),
            pltpu.VMEM((per, LANES), f32),
            pltpu.SemaphoreType.DMA((col_count,)),
            pltpu.SemaphoreType.DMA((col_count,)),
            pltpu.SemaphoreType.DMA((row_count,)),
            pltpu.SemaphoreType.DMA((row_count,)),
        ],
        compiler_params=pltpu.CompilerParams(
            collective_id=0, has_side_effects=True, vmem_limit_bytes=48 * 1024 * 1024
        ),
    )(positions, coefficients, atom_pairs, pair_scale.reshape(1, width))


def solution(mesh):
    in_specs = (P(("row", "col"), None), P(("row", "col"), None), P(), P())
    out_specs = P(("row", "col"), None)
    return jax.shard_map(
        on_device, mesh=mesh, in_specs=in_specs, out_specs=out_specs, check_vma=False
    )
```

```python
import functools
import math

import jax
import jax.numpy as jnp
from jax import lax
from jax.experimental import pallas as pl
from jax.experimental.pallas import tpu as pltpu
from jax.sharding import PartitionSpec as P

length_scale = 2.0
decay_rate = math.sqrt(5.0) / length_scale
outer_factor = decay_rate * decay_rate / 3.0
radial_factor = decay_rate * decay_rate

LANES = 128
HALF = 64
TILE = 256
f32, bf16 = jnp.float32, jnp.bfloat16


def dot(a, b):
    return jnp.dot(a, b, preferred_element_type=f32)


def rounded(v):
    return v.astype(bf16).astype(f32)


def two_parts(v):
    hi = v.astype(bf16)
    return hi, (v - hi.astype(f32)).astype(bf16)


def operands(packed):
    hi = rounded(packed)
    rest = packed - hi
    mid = rounded(rest)
    low = pltpu.roll(rest - mid, HALF, 1)
    first = lax.broadcasted_iota(jnp.int32, packed.shape, 1) < HALF
    hi = hi.astype(bf16)
    for_spans = jnp.concatenate([hi, jnp.where(first, mid, low).astype(bf16)], axis=1)
    for_moves = jnp.concatenate([hi, jnp.where(first, low, mid).astype(bf16)], axis=1)
    return for_spans, for_moves


MESH = pl.DeviceIdType.MESH


def kernel(
    row_count, col_count, per, atoms, width,
    pos_hbm, coef_hbm, pairs_hbm, scale_hbm, out_ref,
    pos_in, coef_in, pairs_in, scale_in, cols, rows, pairs, scale, table_s, table_m,
    row_s, row_x, row_w, row_t, hold_x, hold_u, partial, landed,
    local, send_col, recv_col, send_row, recv_row, send_sum, recv_sum,
):
    row = lax.axis_index("row")
    col = lax.axis_index("col")
    padded = table_s.shape[1]
    block = 3 * per
    count = col_count * per
    tall = row_count * per

    loads = [
        pltpu.make_async_copy(src, dst, local.at[i])
        for i, (src, dst) in enumerate(
            [(pos_hbm, pos_in), (coef_hbm, coef_in), (pairs_hbm, pairs_in), (scale_hbm, scale_in)]
        )
    ]
    for load in loads:
        load.start()
    barrier = pltpu.get_barrier_semaphore()
    for s in range(1, col_count):
        pl.semaphore_signal(
            barrier, inc=1, device_id=(row, lax.rem(col + s, col_count)), device_id_type=MESH
        )
    for k in range(1, row_count):
        pl.semaphore_signal(
            barrier, inc=1, device_id=(lax.rem(row + k, row_count), col), device_id_type=MESH
        )

    loads[0].wait()
    loads[1].wait()
    position, coefficient = pos_in[...], coef_in[...]
    gap = jnp.zeros((per, HALF - atoms), f32)
    for k in range(3):
        cut = slice(k * atoms, (k + 1) * atoms)
        packed = jnp.concatenate([position[:, cut], gap, coefficient[:, cut], gap], axis=1)
        cols[k * per : (k + 1) * per, :] = packed
        rows[k * per : (k + 1) * per, :] = packed

    pl.semaphore_wait(barrier, col_count - 1 + row_count - 1)
    spread = []
    for s in range(1, col_count):
        spread.append(
            pltpu.make_async_remote_copy(
                src_ref=cols.at[pl.ds(0, block)],
                dst_ref=cols.at[pl.ds(s * block, block)],
                send_sem=send_col.at[s],
                recv_sem=recv_col.at[s],
                device_id=(row, lax.rem(col + col_count - s, col_count)),
                device_id_type=MESH,
            )
        )
    shared = []
    for k in range(1, row_count):
        shared.append(
            pltpu.make_async_remote_copy(
                src_ref=rows.at[pl.ds(0, block)],
                dst_ref=rows.at[pl.ds(k * block, block)],
                send_sem=send_row.at[k],
                recv_sem=recv_row.at[k],
                device_id=(lax.rem(row + row_count - k, row_count), col),
                device_id_type=MESH,
            )
        )
    for copy in spread + shared:
        copy.start()

    loads[2].wait()
    loads[3].wait()
    pairs[...] = jnp.full(pairs.shape, -1, jnp.int32)
    pairs[0:2, 0:width] = pairs_in[...]
    scale[...] = jnp.zeros(scale.shape, f32)
    scale[0:1, 0:width] = scale_in[...].reshape(1, width)
    ids = lax.broadcasted_iota(jnp.int32, (HALF, padded), 0)
    signs = (jnp.where(ids == pairs[0:1, :], 1.0, 0.0) - jnp.where(ids == pairs[1:2, :], 1.0, 0.0)).astype(bf16)
    blank = jnp.zeros((HALF, padded), bf16)
    for q in range(4):
        table_s[q * HALF : (q + 1) * HALF, :] = blank if q == 1 else signs
        table_m[q * HALF : (q + 1) * HALF, :] = blank if q == 0 else signs

    def spans_at(for_spans, geoms, t):
        cut = slice(t * TILE, (t + 1) * TILE)
        spans = dot(for_spans, table_s[:, cut])
        parts = spans.reshape(geoms, 3, per, TILE)
        square = parts[:, 0] * parts[:, 0] + parts[:, 1] * parts[:, 1] + parts[:, 2] * parts[:, 2]
        square = square.reshape(geoms * per, TILE)
        if (t + 1) * TILE > width:
            lane = lax.broadcasted_iota(jnp.int32, square.shape, 1)
            square = jnp.where(lane < width - t * TILE, square, 1.0)
        inverse = lax.rsqrt(square)
        features = scale[0:1, cut] * inverse
        return spans, features, features * inverse * inverse

    for copy in shared:
        copy.wait_recv()
    for_spans, _ = operands(rows[...])
    row_square = jnp.zeros((tall, 1), f32)
    for t in range(padded // TILE):
        cut = slice(t * TILE, (t + 1) * TILE)
        spans, features, weights = spans_at(for_spans, row_count, t)
        row_s[:, cut] = spans
        row_x[:, cut] = features
        row_w[:, cut] = weights
        row_square += jnp.sum(features * features, axis=1, keepdims=True)
        hi = rounded(features)
        stacked = [hi, features - hi]
        if row_t.shape[1] > 2 * tall:
            stacked.append(jnp.zeros((row_t.shape[1] - 2 * tall, TILE), f32))
        row_t[cut, :] = jnp.concatenate(stacked, axis=0).T.astype(bf16)

    for copy in spread:
        copy.wait_recv()
    for_spans, for_moves = operands(cols[...])
    square = jnp.zeros((count, LANES), f32)
    mixed = jnp.zeros((count, LANES), f32)
    for t in range(padded // TILE):
        cut = slice(t * TILE, (t + 1) * TILE)
        spans, features, weights = spans_at(for_spans, col_count, t)
        moves = dot(for_moves, table_m[:, cut]).reshape(col_count, 3, per, TILE)
        spans = spans.reshape(col_count, 3, per, TILE)
        inner = spans[:, 0] * moves[:, 0] + spans[:, 1] * moves[:, 1] + spans[:, 2] * moves[:, 2]
        tangents = -weights * inner.reshape(count, TILE)
        for part in range(TILE // LANES):
            x = features[:, part * LANES : (part + 1) * LANES]
            u = tangents[:, part * LANES : (part + 1) * LANES]
            square += x * x
            mixed += x * u
        hi, low = two_parts(features)
        hold_x[0:count, cut] = hi
        hold_x[count : 2 * count, cut] = low
        hi, low = two_parts(tangents)
        hold_u[0:count, cut] = hi
        hold_u[count : 2 * count, cut] = low

    turned = row_t[...]
    gram = dot(hold_x[...], turned)
    gram = (gram[0:count] + gram[count : 2 * count]).T
    gram = gram[0:tall] + gram[tall : 2 * tall]
    cross = dot(hold_u[...], turned)
    cross = (cross[0:count] + cross[count : 2 * count]).T
    cross = cross[0:tall] + cross[tall : 2 * tall]
    square = jnp.sum(square.T, axis=0, keepdims=True)
    mixed = jnp.sum(mixed.T, axis=0, keepdims=True)
    radius = jnp.sqrt(jnp.maximum(row_square + square - 2.0 * gram, 0.0))
    envelope = outer_factor * jnp.exp(-decay_rate * radius)
    direct = envelope * (1.0 + decay_rate * radius)
    bent = radial_factor * (envelope * (cross - mixed))
    bent_sum = jnp.sum(bent, axis=1, keepdims=True)

    def doubled(v):
        hi = rounded(v)
        both = jnp.concatenate([hi, v - hi], axis=0).astype(bf16)
        return jnp.concatenate([both, both], axis=1)

    direct, bent = doubled(direct), doubled(bent)
    result = jnp.zeros((2 * row_count * block, HALF), f32)
    for t in range(padded // TILE):
        cut = slice(t * TILE, (t + 1) * TILE)
        grads = dot(direct, hold_u[:, cut]) + dot(bent, hold_x[:, cut])
        grads = grads[0:tall] + grads[tall : 2 * tall] - bent_sum * row_x[:, cut]
        pulled = -(row_w[:, cut] * grads).reshape(row_count, 1, per, TILE)
        whole = (pulled * row_s[:, cut].reshape(row_count, 3, per, TILE)).reshape(row_count * block, TILE)
        hi, low = two_parts(whole)
        result += lax.dot_general(
            jnp.concatenate([hi, low], axis=0), table_s[0:HALF, cut], (((1,), (1,)), ((), ())),
            preferred_element_type=f32,
        )
    result = result[0 : row_count * block] + result[row_count * block :]

    sums = []
    for k in range(row_count):
        base = k * block
        ends = [result[base + i * per : base + (i + 1) * per, 0:atoms] for i in range(3)]
        ends.append(jnp.zeros((per, partial.shape[2] - 3 * atoms), f32))
        partial[k] = jnp.concatenate(ends, axis=1)
        if k:
            sums.append(
                pltpu.make_async_remote_copy(
                    src_ref=partial.at[k],
                    dst_ref=landed.at[k],
                    send_sem=send_sum.at[k],
                    recv_sem=recv_sum.at[k],
                    device_id=(lax.rem(row + k, row_count), col),
                    device_id_type=MESH,
                )
            )
    for copy in sums:
        copy.start()
    for copy in spread + shared:
        copy.wait_send()
    total = partial[0]
    for k, copy in enumerate(sums):
        copy.wait_recv()
        total += landed[k + 1]
    out_ref[...] = total[:, 0 : 3 * atoms]
    for copy in sums:
        copy.wait_send()


def on_device(positions, coefficients, atom_pairs, pair_scale):
    row_count = lax.axis_size("row")
    col_count = lax.axis_size("col")
    per = positions.shape[0]
    atoms = positions.shape[1] // 3
    width = atom_pairs.shape[1]
    padded = -(-width // TILE) * TILE
    count = col_count * per
    tall = row_count * per
    wide = -(-3 * atoms // LANES) * LANES
    anywhere = pl.BlockSpec(memory_space=pltpu.MemorySpace.HBM)
    return pl.pallas_call(
        functools.partial(kernel, row_count, col_count, per, atoms, width),
        out_shape=jax.ShapeDtypeStruct(positions.shape, f32),
        in_specs=[anywhere] * 4,
        out_specs=pl.BlockSpec(memory_space=pltpu.VMEM),
        scratch_shapes=[
            pltpu.VMEM(positions.shape, f32),
            pltpu.VMEM(coefficients.shape, f32),
            pltpu.VMEM(atom_pairs.shape, jnp.int32),
            pltpu.VMEM(pair_scale.shape, f32),
            pltpu.VMEM((3 * count, LANES), f32),
            pltpu.VMEM((3 * tall, LANES), f32),
            pltpu.VMEM((8, padded), jnp.int32),
            pltpu.VMEM((8, padded), f32),
            pltpu.VMEM((TILE, padded), bf16),
            pltpu.VMEM((TILE, padded), bf16),
            pltpu.VMEM((3 * tall, padded), f32),
            pltpu.VMEM((tall, padded), f32),
            pltpu.VMEM((tall, padded), f32),
            pltpu.VMEM((padded, -(-2 * tall // LANES) * LANES), bf16),
            pltpu.VMEM((2 * count, padded), bf16),
            pltpu.VMEM((2 * count, padded), bf16),
            pltpu.VMEM((row_count, per, wide), f32),
            pltpu.VMEM((row_count, per, wide), f32),
            pltpu.SemaphoreType.DMA((4,)),
            pltpu.SemaphoreType.DMA((col_count,)),
            pltpu.SemaphoreType.DMA((col_count,)),
            pltpu.SemaphoreType.DMA((row_count,)),
            pltpu.SemaphoreType.DMA((row_count,)),
            pltpu.SemaphoreType.DMA((row_count,)),
            pltpu.SemaphoreType.DMA((row_count,)),
        ],
        compiler_params=pltpu.CompilerParams(
            collective_id=0, has_side_effects=True, vmem_limit_bytes=48 * 1024 * 1024
        ),
    )(positions, coefficients, atom_pairs, pair_scale)


def solution(mesh):
    in_specs = (P(("row", "col"), None), P(("row", "col"), None), P(), P())
    out_specs = P(("row", "col"), None)
    return jax.shard_map(
        on_device, mesh=mesh, in_specs=in_specs, out_specs=out_specs, check_vma=False
    )
```

```python
import functools
import math

import jax
import jax.numpy as jnp
from jax import lax
from jax.experimental import pallas as pl
from jax.experimental.pallas import tpu as pltpu
from jax.sharding import PartitionSpec as P

length_scale = 2.0
decay_rate = math.sqrt(5.0) / length_scale
outer_factor = decay_rate * decay_rate / 3.0
radial_factor = decay_rate * decay_rate

LANES = 128
HALF = 64
TILE = 256
f32, bf16 = jnp.float32, jnp.bfloat16


def dot(a, b):
    return jnp.dot(a, b, preferred_element_type=f32)


def rounded(v):
    return v.astype(bf16).astype(f32)


def two_parts(v):
    hi = v.astype(bf16)
    return hi, (v - hi.astype(f32)).astype(bf16)


def operands(packed):
    hi = rounded(packed)
    rest = packed - hi
    mid = rounded(rest)
    low = pltpu.roll(rest - mid, HALF, 1)
    first = lax.broadcasted_iota(jnp.int32, packed.shape, 1) < HALF
    hi = hi.astype(bf16)
    for_spans = jnp.concatenate([hi, jnp.where(first, mid, low).astype(bf16)], axis=1)
    for_moves = jnp.concatenate([hi, jnp.where(first, low, mid).astype(bf16)], axis=1)
    return for_spans, for_moves


MESH = pl.DeviceIdType.MESH


def plan(row_count, col_count):
    cores = 2 if row_count % 2 == 0 else 1
    sides = 2 if col_count % 2 == 0 else 1
    nears = 2 if (col_count // sides) % 2 == 0 else 1
    fars, ys = col_count // sides // nears, row_count // cores
    summed = [(y, 0, n, x, 0) for y in range(ys) for n in range(nears) for x in range(sides)]
    shared = [(0, f, 0, 0, c) for f in range(fars) for c in range(cores)]
    summed.sort(key=lambda o: sum(v > 0 for v in o))
    shared.sort(key=lambda o: sum(v > 0 for v in o))
    return (ys, fars, nears, sides, cores), summed, shared


def kernel(
    row_count, col_count, per, atoms, width,
    pos_hbm, coef_hbm, pairs_hbm, scale_hbm, out_ref,
    pos_in, coef_in, pairs_in, scale_in, cols, rows, pairs, scale, table_s, table_m,
    row_s, row_x, row_w, row_t, hold_x, hold_u, partial, landed,
    local, send_col, recv_col, send_row, recv_row, send_sum, recv_sum,
):
    row = lax.axis_index("row")
    col = lax.axis_index("col")
    padded = table_s.shape[1]
    block = 3 * per
    sizes, summed, group = plan(row_count, col_count)
    wide_count, tall_count = len(summed), len(group)
    count = wide_count * per
    tall = tall_count * per
    ys, fars, nears, sides, cores = sizes
    here = (row // cores, col // (sides * nears), lax.rem(col // sides, nears), lax.rem(col, sides), lax.rem(row, cores))

    def peer(offset, sign):
        y, far, near, side, core = [
            lax.rem(at + (step if sign > 0 else size - step), size)
            for at, step, size in zip(here, offset, sizes)
        ]
        return (y * cores + core, (far * nears + near) * sides + side)

    loads = [
        pltpu.make_async_copy(src, dst, local.at[i])
        for i, (src, dst) in enumerate(
            [(pos_hbm, pos_in), (coef_hbm, coef_in), (pairs_hbm, pairs_in), (scale_hbm, scale_in)]
        )
    ]
    for load in loads:
        load.start()
    barrier = pltpu.get_barrier_semaphore()
    for offset in summed[1:] + group[1:]:
        pl.semaphore_signal(barrier, inc=1, device_id=peer(offset, 1), device_id_type=MESH)

    loads[0].wait()
    loads[1].wait()
    position, coefficient = pos_in[...], coef_in[...]
    gap = jnp.zeros((per, HALF - atoms), f32)
    for k in range(3):
        cut = slice(k * atoms, (k + 1) * atoms)
        packed = jnp.concatenate([position[:, cut], gap, coefficient[:, cut], gap], axis=1)
        cols[k * per : (k + 1) * per, :] = packed
        rows[k * per : (k + 1) * per, :] = packed

    pl.semaphore_wait(barrier, wide_count - 1 + tall_count - 1)
    spread = []
    for s in reversed(range(1, wide_count)):
        spread.append(
            pltpu.make_async_remote_copy(
                src_ref=cols.at[pl.ds(0, block)],
                dst_ref=cols.at[pl.ds(s * block, block)],
                send_sem=send_col.at[s],
                recv_sem=recv_col.at[s],
                device_id=peer(summed[s], -1),
                device_id_type=MESH,
            )
        )
    shared = []
    for k in range(1, tall_count):
        shared.append(
            pltpu.make_async_remote_copy(
                src_ref=rows.at[pl.ds(0, block)],
                dst_ref=rows.at[pl.ds(k * block, block)],
                send_sem=send_row.at[k],
                recv_sem=recv_row.at[k],
                device_id=peer(group[k], -1),
                device_id_type=MESH,
            )
        )
    for copy in spread + shared:
        copy.start()

    loads[2].wait()
    loads[3].wait()
    pairs[...] = jnp.full(pairs.shape, -1, jnp.int32)
    pairs[0:2, 0:width] = pairs_in[...]
    scale[...] = jnp.zeros(scale.shape, f32)
    scale[0:1, 0:width] = scale_in[...].reshape(1, width)
    ids = lax.broadcasted_iota(jnp.int32, (HALF, padded), 0)
    signs = (jnp.where(ids == pairs[0:1, :], 1.0, 0.0) - jnp.where(ids == pairs[1:2, :], 1.0, 0.0)).astype(bf16)
    blank = jnp.zeros((HALF, padded), bf16)
    for q in range(4):
        table_s[q * HALF : (q + 1) * HALF, :] = blank if q == 1 else signs
        table_m[q * HALF : (q + 1) * HALF, :] = blank if q == 0 else signs

    def spans_at(for_spans, geoms, t):
        cut = slice(t * TILE, (t + 1) * TILE)
        spans = dot(for_spans, table_s[:, cut])
        parts = spans.reshape(geoms, 3, per, TILE)
        square = parts[:, 0] * parts[:, 0] + parts[:, 1] * parts[:, 1] + parts[:, 2] * parts[:, 2]
        square = square.reshape(geoms * per, TILE)
        if (t + 1) * TILE > width:
            lane = lax.broadcasted_iota(jnp.int32, square.shape, 1)
            square = jnp.where(lane < width - t * TILE, square, 1.0)
        inverse = lax.rsqrt(square)
        features = scale[0:1, cut] * inverse
        return spans, features, features * inverse * inverse

    for copy in shared:
        copy.wait_recv()
    for_spans, _ = operands(rows[...])
    row_square = jnp.zeros((tall, 1), f32)
    for t in range(padded // TILE):
        cut = slice(t * TILE, (t + 1) * TILE)
        spans, features, weights = spans_at(for_spans, tall_count, t)
        row_s[:, cut] = spans
        row_x[:, cut] = features
        row_w[:, cut] = weights
        row_square += jnp.sum(features * features, axis=1, keepdims=True)
        hi = rounded(features)
        stacked = [hi, features - hi]
        if row_t.shape[1] > 2 * tall:
            stacked.append(jnp.zeros((row_t.shape[1] - 2 * tall, TILE), f32))
        row_t[cut, :] = jnp.concatenate(stacked, axis=0).T.astype(bf16)

    for copy in spread:
        copy.wait_recv()
    for_spans, for_moves = operands(cols[...])
    square = jnp.zeros((count, LANES), f32)
    mixed = jnp.zeros((count, LANES), f32)
    for t in range(padded // TILE):
        cut = slice(t * TILE, (t + 1) * TILE)
        spans, features, weights = spans_at(for_spans, wide_count, t)
        moves = dot(for_moves, table_m[:, cut]).reshape(wide_count, 3, per, TILE)
        spans = spans.reshape(wide_count, 3, per, TILE)
        inner = spans[:, 0] * moves[:, 0] + spans[:, 1] * moves[:, 1] + spans[:, 2] * moves[:, 2]
        tangents = -weights * inner.reshape(count, TILE)
        for part in range(TILE // LANES):
            x = features[:, part * LANES : (part + 1) * LANES]
            u = tangents[:, part * LANES : (part + 1) * LANES]
            square += x * x
            mixed += x * u
        hi, low = two_parts(features)
        hold_x[0:count, cut] = hi
        hold_x[count : 2 * count, cut] = low
        hi, low = two_parts(tangents)
        hold_u[0:count, cut] = hi
        hold_u[count : 2 * count, cut] = low

    turned = row_t[...]
    gram = dot(hold_x[...], turned)
    gram = (gram[0:count] + gram[count : 2 * count]).T
    gram = gram[0:tall] + gram[tall : 2 * tall]
    cross = dot(hold_u[...], turned)
    cross = (cross[0:count] + cross[count : 2 * count]).T
    cross = cross[0:tall] + cross[tall : 2 * tall]
    square = jnp.sum(square.T, axis=0, keepdims=True)
    mixed = jnp.sum(mixed.T, axis=0, keepdims=True)
    radius = jnp.sqrt(jnp.maximum(row_square + square - 2.0 * gram, 0.0))
    envelope = outer_factor * jnp.exp(-decay_rate * radius)
    direct = envelope * (1.0 + decay_rate * radius)
    bent = radial_factor * (envelope * (cross - mixed))
    bent_sum = jnp.sum(bent, axis=1, keepdims=True)

    def doubled(v):
        hi = rounded(v)
        both = jnp.concatenate([hi, v - hi], axis=0).astype(bf16)
        return jnp.concatenate([both, both], axis=1)

    direct, bent = doubled(direct), doubled(bent)
    result = jnp.zeros((2 * tall_count * block, HALF), f32)
    for t in range(padded // TILE):
        cut = slice(t * TILE, (t + 1) * TILE)
        grads = dot(direct, hold_u[:, cut]) + dot(bent, hold_x[:, cut])
        grads = grads[0:tall] + grads[tall : 2 * tall] - bent_sum * row_x[:, cut]
        pulled = -(row_w[:, cut] * grads).reshape(tall_count, 1, per, TILE)
        whole = (pulled * row_s[:, cut].reshape(tall_count, 3, per, TILE)).reshape(tall_count * block, TILE)
        hi, low = two_parts(whole)
        result += lax.dot_general(
            jnp.concatenate([hi, low], axis=0), table_s[0:HALF, cut], (((1,), (1,)), ((), ())),
            preferred_element_type=f32,
        )
    result = result[0 : tall_count * block] + result[tall_count * block :]

    sums = []
    for k in range(tall_count):
        r = [result[k * block + i * per : k * block + (i + 1) * per] for i in range(3)]
        partial[k, 0:per] = jnp.concatenate([r[0], r[1]], axis=1)
        partial[k, per:] = jnp.concatenate([r[2][0 : per // 2], r[2][per // 2 :]], axis=1)
        if k:
            sums.append(
                pltpu.make_async_remote_copy(
                    src_ref=partial.at[k],
                    dst_ref=landed.at[k],
                    send_sem=send_sum.at[k],
                    recv_sem=recv_sum.at[k],
                    device_id=peer(group[k], 1),
                    device_id_type=MESH,
                )
            )
    for copy in sums:
        copy.start()
    for copy in spread + shared:
        copy.wait_send()
    total = partial[0]
    for k, copy in enumerate(sums):
        copy.wait_recv()
        total += landed[k + 1]
    first, second, third = total[0:per, 0:atoms], total[0:per, HALF : HALF + atoms], total[per:]
    third = jnp.concatenate([third[:, 0:atoms], third[:, HALF : HALF + atoms]], axis=0)
    out_ref[...] = jnp.concatenate([first, second, third], axis=1)
    for copy in sums:
        copy.wait_send()


def on_device(positions, coefficients, atom_pairs, pair_scale):
    row_count = lax.axis_size("row")
    col_count = lax.axis_size("col")
    per = positions.shape[0]
    atoms = positions.shape[1] // 3
    width = atom_pairs.shape[1]
    padded = -(-width // TILE) * TILE
    _, summed, group = plan(row_count, col_count)
    count = len(summed) * per
    tall = len(group) * per
    anywhere = pl.BlockSpec(memory_space=pltpu.MemorySpace.HBM)
    return pl.pallas_call(
        functools.partial(kernel, row_count, col_count, per, atoms, width),
        out_shape=jax.ShapeDtypeStruct(positions.shape, f32),
        in_specs=[anywhere] * 4,
        out_specs=pl.BlockSpec(memory_space=pltpu.VMEM),
        scratch_shapes=[
            pltpu.VMEM(positions.shape, f32),
            pltpu.VMEM(coefficients.shape, f32),
            pltpu.VMEM(atom_pairs.shape, jnp.int32),
            pltpu.VMEM(pair_scale.shape, f32),
            pltpu.VMEM((3 * count, LANES), f32),
            pltpu.VMEM((3 * tall, LANES), f32),
            pltpu.VMEM((8, padded), jnp.int32),
            pltpu.VMEM((8, padded), f32),
            pltpu.VMEM((TILE, padded), bf16),
            pltpu.VMEM((TILE, padded), bf16),
            pltpu.VMEM((3 * tall, padded), f32),
            pltpu.VMEM((tall, padded), f32),
            pltpu.VMEM((tall, padded), f32),
            pltpu.VMEM((padded, -(-2 * tall // LANES) * LANES), bf16),
            pltpu.VMEM((2 * count, padded), bf16),
            pltpu.VMEM((2 * count, padded), bf16),
            pltpu.VMEM((len(group), 3 * per // 2, LANES), f32),
            pltpu.VMEM((len(group), 3 * per // 2, LANES), f32),
            pltpu.SemaphoreType.DMA((4,)),
            pltpu.SemaphoreType.DMA((len(summed),)),
            pltpu.SemaphoreType.DMA((len(summed),)),
            pltpu.SemaphoreType.DMA((len(group),)),
            pltpu.SemaphoreType.DMA((len(group),)),
            pltpu.SemaphoreType.DMA((len(group),)),
            pltpu.SemaphoreType.DMA((len(group),)),
        ],
        compiler_params=pltpu.CompilerParams(
            collective_id=0, has_side_effects=True, vmem_limit_bytes=60 * 1024 * 1024
        ),
    )(positions, coefficients, atom_pairs, pair_scale)


def solution(mesh):
    in_specs = (P(("row", "col"), None), P(("row", "col"), None), P(), P())
    out_specs = P(("row", "col"), None)
    return jax.shard_map(
        on_device, mesh=mesh, in_specs=in_specs, out_specs=out_specs, check_vma=False
    )
```

```python
import functools
import math

import jax
import jax.numpy as jnp
from jax import lax
from jax.experimental import pallas as pl
from jax.experimental.pallas import tpu as pltpu
from jax.sharding import PartitionSpec as P

length_scale = 2.0
decay_rate = math.sqrt(5.0) / length_scale
outer_factor = decay_rate * decay_rate / 3.0
radial_factor = decay_rate * decay_rate

LANES = 128
HALF = 64
TILE = 256
f32, bf16 = jnp.float32, jnp.bfloat16


def dot(a, b):
    return jnp.dot(a, b, preferred_element_type=f32)


def rounded(v):
    return v.astype(bf16).astype(f32)


def two_parts(v):
    hi = v.astype(bf16)
    return hi, (v - hi.astype(f32)).astype(bf16)


def operands(packed):
    hi = rounded(packed)
    rest = packed - hi
    mid = rounded(rest)
    low = pltpu.roll(rest - mid, HALF, 1)
    first = lax.broadcasted_iota(jnp.int32, packed.shape, 1) < HALF
    hi = hi.astype(bf16)
    for_spans = jnp.concatenate([hi, jnp.where(first, mid, low).astype(bf16)], axis=1)
    for_moves = jnp.concatenate([hi, jnp.where(first, low, mid).astype(bf16)], axis=1)
    return for_spans, for_moves


MESH = pl.DeviceIdType.MESH


def plan(row_count, col_count):
    cores = 2 if row_count % 2 == 0 else 1
    sides = 2 if col_count % 2 == 0 else 1
    nears = 2 if (col_count // sides) % 2 == 0 else 1
    fars, ys = col_count // sides // nears, row_count // cores
    summed = [(y, 0, n, x, 0) for y in range(ys) for n in range(nears) for x in range(sides)]
    shared = [(0, f, 0, 0, c) for f in range(fars) for c in range(cores)]
    summed.sort(key=lambda o: sum(v > 0 for v in o))
    shared.sort(key=lambda o: sum(v > 0 for v in o))
    return (ys, fars, nears, sides, cores), summed, shared


def kernel(
    row_count, col_count, per, atoms, width,
    pos_hbm, coef_hbm, pairs_hbm, scale_hbm, out_ref,
    pos_in, coef_in, pairs_in, scale_in, cols, rows, pairs, scale, table_s, table_m,
    row_s, row_x, row_w, row_t, hold_x, hold_u, partial, landed,
    local, send_col, recv_col, send_row, recv_row, send_sum, recv_sum,
):
    row = lax.axis_index("row")
    col = lax.axis_index("col")
    padded = table_s.shape[1]
    block = 3 * per
    sizes, summed, group = plan(row_count, col_count)
    wide_count, tall_count = len(summed), len(group)
    count = wide_count * per
    tall = tall_count * per
    ys, fars, nears, sides, cores = sizes
    here = (row // cores, col // (sides * nears), lax.rem(col // sides, nears), lax.rem(col, sides), lax.rem(row, cores))

    def peer(offset, sign):
        y, far, near, side, core = [
            lax.rem(at + (step if sign > 0 else size - step), size)
            for at, step, size in zip(here, offset, sizes)
        ]
        return (y * cores + core, (far * nears + near) * sides + side)

    loads = [
        pltpu.make_async_copy(src, dst, local.at[i])
        for i, (src, dst) in enumerate(
            [(pos_hbm, pos_in), (coef_hbm, coef_in), (pairs_hbm, pairs_in), (scale_hbm, scale_in)]
        )
    ]
    for load in loads:
        load.start()
    barrier = pltpu.get_barrier_semaphore()
    for offset in summed[1:] + group[1:]:
        pl.semaphore_signal(barrier, inc=1, device_id=peer(offset, 1), device_id_type=MESH)

    loads[0].wait()
    loads[1].wait()
    position, coefficient = pos_in[...], coef_in[...]
    gap = jnp.zeros((per, HALF - atoms), f32)
    part = per // 2
    short = 3 * part
    for k in range(3):
        cut = slice(k * atoms, (k + 1) * atoms)
        packed = jnp.concatenate([position[:, cut], gap, coefficient[:, cut], gap], axis=1)
        cols[k * per : (k + 1) * per, :] = packed
        rows[k * part : (k + 1) * part, :] = jnp.concatenate(
            [position[0:part, cut], gap[0:part], position[part:, cut], gap[0:part]], axis=1
        )

    pl.semaphore_wait(barrier, wide_count - 1 + tall_count - 1)
    spread = {}
    for s in range(1, wide_count):
        spread[s] = pltpu.make_async_remote_copy(
            src_ref=cols.at[pl.ds(0, block)],
            dst_ref=cols.at[pl.ds(s * block, block)],
            send_sem=send_col.at[s],
            recv_sem=recv_col.at[s],
            device_id=peer(summed[s], -1),
            device_id_type=MESH,
        )
    shared = []
    for k in range(1, tall_count):
        shared.append(
            pltpu.make_async_remote_copy(
                src_ref=rows.at[pl.ds(0, short)],
                dst_ref=rows.at[pl.ds(k * short, short)],
                send_sem=send_row.at[k],
                recv_sem=recv_row.at[k],
                device_id=peer(group[k], -1),
                device_id_type=MESH,
            )
        )
    for copy in list(spread.values()) + shared:
        copy.start()

    loads[2].wait()
    loads[3].wait()
    pairs[...] = jnp.full(pairs.shape, -1, jnp.int32)
    pairs[0:2, 0:width] = pairs_in[...]
    scale[...] = jnp.zeros(scale.shape, f32)
    scale[0:1, 0:width] = scale_in[...].reshape(1, width)
    ids = lax.broadcasted_iota(jnp.int32, (HALF, padded), 0)
    signs = (jnp.where(ids == pairs[0:1, :], 1.0, 0.0) - jnp.where(ids == pairs[1:2, :], 1.0, 0.0)).astype(bf16)
    blank = jnp.zeros((HALF, padded), bf16)
    for q in range(4):
        table_s[q * HALF : (q + 1) * HALF, :] = blank if q == 1 else signs
        table_m[q * HALF : (q + 1) * HALF, :] = blank if q == 0 else signs

    def terms(parts, geoms, t):
        cut = slice(t * TILE, (t + 1) * TILE)
        square = parts[:, 0] * parts[:, 0] + parts[:, 1] * parts[:, 1] + parts[:, 2] * parts[:, 2]
        square = square.reshape(geoms * per, TILE)
        if (t + 1) * TILE > width:
            lane = lax.broadcasted_iota(jnp.int32, square.shape, 1)
            square = jnp.where(lane < width - t * TILE, square, 1.0)
        inverse = lax.rsqrt(square)
        features = scale[0:1, cut] * inverse
        return features, features * inverse * inverse

    def summed_terms(low, high):
        many = high - low
        size, base = many * per, 2 * low * per
        for_spans, for_moves = operands(cols[low * block : high * block, :])
        square = jnp.zeros((size, LANES), f32)
        mixed = jnp.zeros((size, LANES), f32)
        for t in range(padded // TILE):
            cut = slice(t * TILE, (t + 1) * TILE)
            spans = dot(for_spans, table_s[:, cut]).reshape(many, 3, per, TILE)
            moves = dot(for_moves, table_m[:, cut]).reshape(many, 3, per, TILE)
            features, weights = terms(spans, many, t)
            inner = spans[:, 0] * moves[:, 0] + spans[:, 1] * moves[:, 1] + spans[:, 2] * moves[:, 2]
            tangents = -weights * inner.reshape(size, TILE)
            for lane in range(0, TILE, LANES):
                x = features[:, lane : lane + LANES]
                u = tangents[:, lane : lane + LANES]
                square += x * x
                mixed += x * u
            for hold, value in ((hold_x, features), (hold_u, tangents)):
                hi, rest = two_parts(value)
                hold[base : base + size, cut] = hi
                hold[base + size : base + 2 * size, cut] = rest
        return jnp.sum(square.T, axis=0, keepdims=True), jnp.sum(mixed.T, axis=0, keepdims=True)

    def doubled(v):
        hi = rounded(v)
        both = jnp.concatenate([hi, v - hi], axis=0).astype(bf16)
        return [both, both]

    def coupled(low, high, square, mixed):
        size, base = (high - low) * per, 2 * low * per
        turned = row_t[...]

        def against(hold):
            both = dot(hold[base : base + 2 * size, :], turned)
            both = (both[0:size] + both[size : 2 * size]).T
            return both[0:tall] + both[tall : 2 * tall]

        radius = jnp.sqrt(jnp.maximum(row_square + square - 2.0 * against(hold_x), 0.0))
        envelope = outer_factor * jnp.exp(-decay_rate * radius)
        direct = envelope * (1.0 + decay_rate * radius)
        bent = radial_factor * (envelope * (against(hold_u) - mixed))
        return doubled(direct), doubled(bent), jnp.sum(bent, axis=1, keepdims=True)

    half = (wide_count + 1) // 2
    for s in range(1, half):
        spread[s].wait_recv()
    near_sums = summed_terms(0, half)

    for copy in shared:
        copy.wait_recv()
    lower, upper = operands(rows[...])
    row_square = jnp.zeros((tall, 1), f32)
    for t in range(padded // TILE):
        cut = slice(t * TILE, (t + 1) * TILE)
        halves = [dot(lower, table_s[:, cut]), dot(upper, table_m[:, cut])]
        spans = jnp.concatenate([v.reshape(tall_count, 3, part, TILE) for v in halves], axis=2)
        features, weights = terms(spans, tall_count, t)
        row_s[:, cut] = spans.reshape(3 * tall, TILE)
        row_x[:, cut] = features
        row_w[:, cut] = weights
        row_square += jnp.sum(features * features, axis=1, keepdims=True)
        hi = rounded(features)
        stacked = [hi, features - hi]
        if row_t.shape[1] > 2 * tall:
            stacked.append(jnp.zeros((row_t.shape[1] - 2 * tall, TILE), f32))
        row_t[cut, :] = jnp.concatenate(stacked, axis=0).T.astype(bf16)

    direct, bent, bent_sum = coupled(0, half, *near_sums)
    if half < wide_count:
        for s in range(half, wide_count):
            spread[s].wait_recv()
        more = coupled(half, wide_count, *summed_terms(half, wide_count))
        direct, bent, bent_sum = direct + more[0], bent + more[1], bent_sum + more[2]
    direct, bent = jnp.concatenate(direct, axis=1), jnp.concatenate(bent, axis=1)
    result = jnp.zeros((2 * tall_count * block, HALF), f32)
    for t in range(padded // TILE):
        cut = slice(t * TILE, (t + 1) * TILE)
        grads = dot(direct, hold_u[:, cut]) + dot(bent, hold_x[:, cut])
        grads = grads[0:tall] + grads[tall : 2 * tall] - bent_sum * row_x[:, cut]
        pulled = -(row_w[:, cut] * grads).reshape(tall_count, 1, per, TILE)
        whole = (pulled * row_s[:, cut].reshape(tall_count, 3, per, TILE)).reshape(tall_count * block, TILE)
        hi, low = two_parts(whole)
        result += lax.dot_general(
            jnp.concatenate([hi, low], axis=0), table_s[0:HALF, cut], (((1,), (1,)), ((), ())),
            preferred_element_type=f32,
        )
    result = result[0 : tall_count * block] + result[tall_count * block :]

    sums = []
    for k in range(tall_count):
        r = [result[k * block + i * per : k * block + (i + 1) * per] for i in range(3)]
        partial[k, 0:per] = jnp.concatenate([r[0], r[1]], axis=1)
        partial[k, per:] = jnp.concatenate([r[2][0 : per // 2], r[2][per // 2 :]], axis=1)
        if k:
            sums.append(
                pltpu.make_async_remote_copy(
                    src_ref=partial.at[k],
                    dst_ref=landed.at[k],
                    send_sem=send_sum.at[k],
                    recv_sem=recv_sum.at[k],
                    device_id=peer(group[k], 1),
                    device_id_type=MESH,
                )
            )
    for copy in sums:
        copy.start()
    for copy in list(spread.values()) + shared:
        copy.wait_send()
    total = partial[0]
    for k, copy in enumerate(sums):
        copy.wait_recv()
        total += landed[k + 1]
    first, second, third = total[0:per, 0:atoms], total[0:per, HALF : HALF + atoms], total[per:]
    third = jnp.concatenate([third[:, 0:atoms], third[:, HALF : HALF + atoms]], axis=0)
    out_ref[...] = jnp.concatenate([first, second, third], axis=1)
    for copy in sums:
        copy.wait_send()


def on_device(positions, coefficients, atom_pairs, pair_scale):
    row_count = lax.axis_size("row")
    col_count = lax.axis_size("col")
    per = positions.shape[0]
    atoms = positions.shape[1] // 3
    width = atom_pairs.shape[1]
    padded = -(-width // TILE) * TILE
    _, summed, group = plan(row_count, col_count)
    count = len(summed) * per
    tall = len(group) * per
    anywhere = pl.BlockSpec(memory_space=pltpu.MemorySpace.HBM)
    return pl.pallas_call(
        functools.partial(kernel, row_count, col_count, per, atoms, width),
        out_shape=jax.ShapeDtypeStruct(positions.shape, f32),
        in_specs=[anywhere] * 4,
        out_specs=pl.BlockSpec(memory_space=pltpu.VMEM),
        scratch_shapes=[
            pltpu.VMEM(positions.shape, f32),
            pltpu.VMEM(coefficients.shape, f32),
            pltpu.VMEM(atom_pairs.shape, jnp.int32),
            pltpu.VMEM(pair_scale.shape, f32),
            pltpu.VMEM((3 * count, LANES), f32),
            pltpu.VMEM((3 * tall // 2, LANES), f32),
            pltpu.VMEM((8, padded), jnp.int32),
            pltpu.VMEM((8, padded), f32),
            pltpu.VMEM((TILE, padded), bf16),
            pltpu.VMEM((TILE, padded), bf16),
            pltpu.VMEM((3 * tall, padded), f32),
            pltpu.VMEM((tall, padded), f32),
            pltpu.VMEM((tall, padded), f32),
            pltpu.VMEM((padded, -(-2 * tall // LANES) * LANES), bf16),
            pltpu.VMEM((2 * count, padded), bf16),
            pltpu.VMEM((2 * count, padded), bf16),
            pltpu.VMEM((len(group), 3 * per // 2, LANES), f32),
            pltpu.VMEM((len(group), 3 * per // 2, LANES), f32),
            pltpu.SemaphoreType.DMA((4,)),
            pltpu.SemaphoreType.DMA((len(summed),)),
            pltpu.SemaphoreType.DMA((len(summed),)),
            pltpu.SemaphoreType.DMA((len(group),)),
            pltpu.SemaphoreType.DMA((len(group),)),
            pltpu.SemaphoreType.DMA((len(group),)),
            pltpu.SemaphoreType.DMA((len(group),)),
        ],
        compiler_params=pltpu.CompilerParams(
            collective_id=0, has_side_effects=True, vmem_limit_bytes=40 * 1024 * 1024
        ),
    )(*[pltpu.with_memory_space_constraint(v, pltpu.MemorySpace.HBM) for v in (positions, coefficients, atom_pairs, pair_scale)])


def solution(mesh):
    in_specs = (P(("row", "col"), None), P(("row", "col"), None), P(), P())
    out_specs = P(("row", "col"), None)
    return jax.shard_map(
        on_device, mesh=mesh, in_specs=in_specs, out_specs=out_specs, check_vma=False
    )
```
